32 devices in a mesh: row: 8 (over z, core), col: 4 (over y, x).
Axes of the slice: x: 2, y: 2, z: 4, core: 2. Of those that a mesh axis runs over, the one named last changes fastest.
Arguments:
- density: bfloat16 [8192, 8192], P('row', 'col'), may hold values from -6 to 6
- listed: int32 [64, 64], P('row', 'col'), may hold values 0 or 1
- three_centre: bfloat16 [128, 512, 512], P(('row', 'col')), may hold values from -0.25 to 0.25
Outputs:
- exchange_diag: float32 [8192, 512], P('row', 'col')
- exchange_density: bfloat16 [8192, 8192], P('row', 'col')
The draws below stay inside these ranges and needn't reach their ends.
All inputs are finite; a program needn't handle non-finite values. No bound on the sum of `listed` on one device may be relied on, other than what follows from the above.
Results may differ from the reference program's by a relative error of at most 0.0058.
Values may be sent and summed in bfloat16 or wider, within the bound.
A program may use at most 64 MiB of HBM per device.

```python
import jax
import jax.numpy as jnp
from jax import lax

TILE = 128
NT = 64
NB = 8192
W = 512
AUX_DEV = 4
TR = 8
NGS = 2
AUX = 128
AUX_GROUP = 8
N_COL = 4


def plant(result, key, least, high):
    place = [jax.random.randint(jax.random.fold_in(key, axis), (), 0, length) for axis, length in enumerate(result.shape)]
    widest = result.shape.index(max(result.shape))
    next_to = place[:widest] + [(place[widest] + 1) % result.shape[widest]] + place[widest + 1:]
    return result.at[tuple(place)].set(least).at[tuple(next_to)].set(high)


def block_scale(stream_key, shape, pieces, smallest, high):
    factor_of, own = 1.0, jax.random.fold_in(stream_key, 6)
    for position, shards_of in pieces:
        heights = jnp.exp(jax.random.uniform(jax.random.fold_in(own, position), (shards_of,), jnp.float32, smallest / len(pieces), high / len(pieces)))
        factor_of = factor_of * jnp.repeat(heights, shape[position] // shards_of).reshape([-1 if axis == position else 1 for axis in range(len(shape))])
    return factor_of


def normal_values(key, dims, scale, most, cuts=(), held_as=jnp.bfloat16):
    array = scale * jax.random.normal(key, dims, jnp.float32)
    if cuts:
        array = array * block_scale(key, dims, cuts, -0.22, 0.18)
    return jnp.clip(array, -most, most).astype(held_as)


def setup_inputs(seed: int = 0) -> dict:
    key_list = jax.random.split(jax.random.key(seed), 4)
    density = normal_values(key_list[0], (NB, NB), 1.0, 6.0, ((0, 8), (1, 4)))
    listed = plant((jax.random.randint(key_list[1], (NT, NT), 0, 2) < 1).astype(jnp.int32), jax.random.fold_in(key_list[1], 1), 0, 1)
    three_centre = normal_values(key_list[2], (AUX, W, W), W ** -0.5, 0.25, ((0, 32),))
    return dict(density=density, listed=listed, three_centre=three_centre)


def reference(density, listed, three_centre):
    masked = (density.reshape(NT, TILE, NT, TILE) * listed[:, None, :, None].astype(jnp.bfloat16)).reshape(NB, NB)
    group_total = NT // 4
    aux_index = jnp.arange(AUX, dtype=jnp.int32)
    device = aux_index // AUX_DEV
    row_pos = device // N_COL
    col_pos = device % N_COL
    aux_slot = aux_index % AUX_DEV
    support = ((row_pos * TR) // 4 + (col_pos * AUX_DEV + aux_slot) % NGS).astype(jnp.int32)

    def accumulate(blocks, item):
        aux_block, group_id = item
        start = (group_id * W).astype(jnp.int32)
        density_sub = lax.dynamic_slice(masked, (start, start), (W, W))
        half_product = jnp.dot(aux_block, density_sub, preferred_element_type=jnp.float32).astype(jnp.bfloat16)
        contribution = jnp.dot(half_product, aux_block.T, preferred_element_type=jnp.float32)
        return blocks.at[group_id].add(contribution), None

    blocks, _ = lax.scan(accumulate, jnp.zeros((group_total, W, W), jnp.float32), (three_centre, support))
    blocks = blocks * (AUX_GROUP ** -0.5)
    exchange_diag = blocks.reshape(NB, W)
    rounded = blocks.astype(jnp.bfloat16)

    def apply_group(group_id):
        dens_rows = lax.dynamic_slice_in_dim(masked, (group_id * W).astype(jnp.int32), W, 0)
        product = jnp.dot(rounded[group_id], dens_rows, preferred_element_type=jnp.float32) * (W ** -0.5)
        return product.astype(jnp.bfloat16)

    exchange_density = lax.map(apply_group, jnp.arange(group_total, dtype=jnp.int32)).reshape(NB, NB)
    return exchange_diag, exchange_density
```

```python
import functools

import jax
import jax.numpy as jnp
from jax import lax
from jax.experimental import pallas as pl
from jax.experimental.pallas import tpu as pltpu
from jax.sharding import PartitionSpec as P

TILE = 128
W = 512
SUP = W // TILE
UNIT = W // 2
STRIP = W // 2
PART = UNIT // 2
PIECE = 64
HALF = W // 2
DIRECT = (0, 3)
BAND = 512
VMEM_GRANT = 32 * 2**20
MESH = pl.DeviceIdType.MESH


def from_root(value, axis, root):
    mine = lax.axis_index(axis) == root
    return lax.psum(jnp.where(mine, value, jnp.zeros_like(value)), axis)


def partner_2(block, axis, stride):
    count = lax.axis_size(axis)
    route = []
    for low in range(count):
        high = low | 1 << stride
        if high != low and high < count:
            route += [(low, high), (high, low)]
    return lax.ppermute(block, axis, route)


def halve_rows(values, row_index, levels, sender):
    for bit_level in reversed(range(levels)):
        middle = values.shape[0] // 2
        lower_half = row_index // 2**bit_level % 2 == 0
        kept_rows = jnp.where(lower_half, values[:middle], values[middle:])
        sent_rows = jnp.where(lower_half, values[middle:], values[:middle])
        values = kept_rows + sender(sent_rows, bit_level)
    return values


def per_device(density, listed, three_centre):
    tile_rows = listed.shape[0]
    tile_cols = listed.shape[1]
    quad_tiles = max(tile_rows, 4)
    groups_dev = quad_tiles // 4
    aux_count = three_centre.shape[0]
    col_count = lax.axis_size("col")
    row_index = lax.axis_index("row")
    col_index = lax.axis_index("col")
    masked = (
        density.reshape(tile_rows, TILE, tile_cols, TILE)
        * listed[:, None, :, None].astype(jnp.bfloat16)
    ).reshape(tile_rows * TILE, tile_cols * TILE)
    quad_start = row_index * tile_rows // quad_tiles * quad_tiles
    col_offset = quad_start % tile_cols * TILE
    portion = lax.dynamic_slice_in_dim(masked, col_offset, quad_tiles * TILE, 1)
    diagonal = from_root(portion, "col", quad_start // tile_cols)
    joined = jnp.concatenate([diagonal, masked], axis=1)
    levels = (quad_tiles // tile_rows).bit_length() - 1
    for bit_level in range(levels):
        partner = partner_2(joined, "row", bit_level)
        lower_half = row_index // 2**bit_level % 2 == 0
        joined = jnp.where(
            lower_half,
            jnp.concatenate([joined, partner], axis=0),
            jnp.concatenate([partner, joined], axis=0),
        )
    quad_block = joined[:, : quad_tiles * TILE]
    quad_density = joined[:, quad_tiles * TILE :]
    group_ids = jnp.arange(groups_dev, dtype=jnp.int32)
    exchange_quad = jnp.zeros((groups_dev, W, W), jnp.float32)
    for aux_slot in range(aux_count):
        group_slot = (col_index * aux_count + aux_slot) % groups_dev
        density_sub = lax.dynamic_slice(quad_block, (group_slot * W, group_slot * W), (W, W))
        aux_block = three_centre[aux_slot]
        half_product = jnp.dot(aux_block, density_sub, preferred_element_type=jnp.float32).astype(
            jnp.bfloat16
        )
        contribution = lax.dot_general(
            half_product, aux_block, (((1,), (1,)), ((), ())), preferred_element_type=jnp.float32
        )
        exchange_quad = exchange_quad + jnp.where(
            (group_ids == group_slot)[:, None, None], contribution[None], 0.0
        )
    aux_group = aux_count * col_count * 4 // tile_rows
    exchange_quad = (exchange_quad * aux_group ** (-0.5)).reshape(quad_tiles * TILE, W)
    column_share = lax.psum_scatter(exchange_quad, "col", scatter_dimension=1, tiled=True)
    exchange_diag = halve_rows(
        column_share,
        row_index,
        levels,
        lambda sent_rows, bit_level: partner_2(sent_rows, "row", bit_level),
    )
    fock_rounded = lax.all_gather(exchange_diag.astype(jnp.bfloat16), "col", axis=1, tiled=True)
    rows_here = tile_rows * TILE
    segment_rows = min(rows_here, W)
    segment_count = rows_here // segment_rows
    within_quad = (row_index * tile_rows - quad_start) * TILE
    products = []
    for segment in range(segment_count):
        group_position = (within_quad + segment * segment_rows) // W
        dens_rows = lax.dynamic_slice_in_dim(quad_density, group_position * W, W, 0)
        fock_part = fock_rounded[segment * segment_rows : (segment + 1) * segment_rows]
        products.append(
            jnp.dot(fock_part, dens_rows, preferred_element_type=jnp.float32) * W ** (-0.5)
        )
    exchange_density = jnp.concatenate(products, axis=0).astype(jnp.bfloat16)
    return (exchange_diag, exchange_density)


def mask_tile(tile, flag):
    return tile * jnp.full(tile.shape, flag.astype(jnp.float32)).astype(jnp.bfloat16)


def exchange_kernel(
    scale, listed, density, three_centre, early, masked_last, fock_last, diag,
    raw, block, coef, half, partial, send_1, recv_1, send_2, recv_2, fock, masked,
    raw_sem, coef_sem, dens_sem, bc_send, bc_recv, twin_send, rs1_send, rs1_recv,
    rs2_send, rs2_recv, ag1_send, ag1_recv, ag2_send, ag2_recv,
):
    tile_rows, tile_cols = listed.shape
    groups = tile_rows // SUP
    per_group = W // UNIT
    units = groups * per_group
    aux_count = three_centre.shape[0]
    row = lax.axis_index("row")
    me = lax.axis_index("col")
    x, y = me % 2, me // 2
    xn, yn = me + 1 - 2 * x, me + 2 - 4 * y
    far = xn + yn - me
    near = (xn, yn)
    first_tile = row * tile_rows
    owner = first_tile // tile_cols
    tile_off = first_tile % tile_cols
    ox, oy = owner % 2, owner // 2
    rx, ry = (x + ox) % 2, (y + oy) % 2
    even = (rx + ry + 1) % 2
    is_owner = rx + ry == 0
    is_far = rx + ry == 2
    hop_to = (xn * even + yn * (1 - even), yn * even + xn * (1 - even))
    last_of = (rx + 2 * (1 - ry) == 0, ry + 2 * (1 - rx) == 0)
    relays_of = (
        (rx + ry) * (rx + 1 - ry) > 0,
        (rx + ry) * (ry + 1 - rx) > 0,
    )
    lead = ry * (1 - rx)

    def remote(src, dst, send_sem, recv_sem, target):
        return pltpu.make_async_remote_copy(
            src_ref=src, dst_ref=dst, send_sem=send_sem, recv_sem=recv_sem,
            device_id=(row, target), device_id_type=MESH,
        )

    def raw_copy(g, p):
        start = (tile_off + g * SUP) * TILE + p * HALF
        columns = pl.ds(pl.multiple_of(start, TILE), HALF)
        return pltpu.make_async_copy(
            density.at[pl.ds(g * W, W), columns], raw.at[g, p], raw_sem.at[g, p]
        )

    def coef_copy(q):
        return pltpu.make_async_copy(three_centre.at[q], coef.at[q], coef_sem.at[q])

    def masked_of(g):
        return masked.at[g] if g < groups - 1 else masked_last

    def dens_copy(g):
        return pltpu.make_async_copy(
            density.at[pl.ds(g * W, W)], masked_of(g), dens_sem.at[g]
        )

    pieces = W // PIECE

    def piece(g, p, i):
        part = block.at[g, p, pl.ds(i * PIECE, PIECE)]
        return remote(part, part, bc_send.at[g, p, i], bc_recv.at[g, p, i], hop_to[p])

    def direct(g, i):
        return i >= pieces - (DIRECT[1] if g == groups - 1 else DIRECT[0]) * W // PIECE // 8

    def twin(g, p, i):
        part = block.at[g, p, pl.ds(i * PIECE, PIECE)]
        return remote(part, part, twin_send.at[g, p, i], bc_recv.at[g, p, i], hop_to[1 - p])

    @pl.when(is_owner)
    def _():
        for g in range(groups):
            for p in range(2):
                raw_copy(g, p).start()

    barrier = pltpu.get_barrier_semaphore()
    for neighbour in near:
        pl.semaphore_signal(barrier, inc=1, device_id=(row, neighbour), device_id_type=MESH)
    for q in range(aux_count):
        coef_copy(q).start()
    for g in range(groups):
        dens_copy(g).start()
    pl.semaphore_wait(barrier, 2)

    @pl.when(is_owner)
    def _():
        for g in range(groups):
            for p in range(2):
                raw_copy(g, p).wait()
            for i in range(pieces):
                rows = pl.ds(i * PIECE, PIECE)
                for p in range(2):
                    for j in range(HALF // TILE):
                        cols = pl.ds(j * TILE, TILE)
                        tile_col = tile_off + g * SUP + p * (HALF // TILE) + j
                        flag = listed[g * SUP + i * PIECE // TILE, tile_col]
                        block[g, p, rows, cols] = mask_tile(raw[g, p, rows, cols], flag)
                    piece(g, p, i).start()
                if direct(g, i):
                    for p in range(2):
                        twin(g, p, i).start()

    def sends(g, p, i):
        if direct(g, i):
            return relays_of[p] & jnp.logical_not(is_far)
        return relays_of[p]

    def relay(g, i):
        for p in range(2):
            @pl.when(sends(g, p, i))
            def _():
                piece(g, p, i).wait_recv()
                piece(g, p, i).start()

    def await_far(g):
        @pl.when(is_far)
        def _():
            for i in range(pieces):
                if direct(g, i):
                    for p in range(2):
                        piece(g, p, i).wait_recv()

    def await_last(g):
        for p in range(2):
            @pl.when(last_of[p])
            def _():
                for i in range(pieces):
                    piece(g, p, i).wait_recv()

    def stage_1(u, h):
        return remote(send_1.at[u, h], recv_1.at[u, h], rs1_send.at[u, h], rs1_recv.at[u, h], near[h])

    def stage_2(u, h):
        return remote(
            send_2.at[u, h], recv_2.at[u, h], rs2_send.at[u, h], rs2_recv.at[u, h], near[1 - h]
        )

    def columns_of(dev):
        return pl.ds(pl.multiple_of(dev * TILE, TILE), TILE)

    def rows_of(u, h):
        return pl.ds(u * UNIT + h * PART, PART)

    def fock_of(u):
        if u < units - per_group:
            return fock, u
        return fock_last, u - (units - per_group)

    def gather_1(u, axis):
        ref, v = fock_of(u)
        part = ref.at[pl.ds(v * UNIT, UNIT), columns_of(me)]
        return remote(part, part, ag1_send.at[u, axis], ag1_recv.at[u, axis], near[axis])

    def gather_2(u, axis):
        ref, v = fock_of(u)
        part = ref.at[rows_of(v, axis), columns_of(near[1 - axis])]
        return remote(part, part, ag2_send.at[u, axis], ag2_recv.at[u, axis], near[axis])

    def members(g):
        return list(range(g, aux_count, groups))

    def columns_half(p):
        return pl.ds(pl.multiple_of(p * HALF, HALF), HALF)

    def first_products(g, p):
        for n, q in enumerate(members(g)):
            yield lambda n=n, q=q: half.__setitem__(
                n, jnp.dot(coef[q], block[g, p], preferred_element_type=jnp.float32).astype(jnp.bfloat16)
            )

    def second_product(g, p, v, fresh):
        rows = pl.ds(v * STRIP, STRIP)
        total = None
        for n, q in enumerate(members(g)):
            term = lax.dot_general(
                half[n, rows], coef[q, :, columns_half(p)], (((1,), (1,)), ((), ())),
                preferred_element_type=jnp.float32,
            )
            total = term if total is None else total + term
        at = pl.ds(g * W + v * STRIP, STRIP)
        if fresh:
            partial[at] = total
        else:
            partial[at] += total

    def send_unit(u):
        for h in range(2):
            send_1[u, h, 0] = partial[rows_of(u, h), columns_of(near[h])].astype(jnp.bfloat16)
            send_1[u, h, 1] = partial[rows_of(u, h), columns_of(far)].astype(jnp.bfloat16)
            stage_1(u, h).start()

    def lead_work(g):
        yield from first_products(g, lead)
        for v in range(W // STRIP):
            yield lambda v=v: second_product(g, lead, v, True)

    def trail_work(g):
        yield from first_products(g, 1 - lead)
        for v in range(W // STRIP):
            def step(v=v):
                second_product(g, 1 - lead, v, False)
                for u in range(v * STRIP // UNIT, (v + 1) * STRIP // UNIT):
                    send_unit(g * per_group + u)
            yield step

    def mask_rows(g):
        for t in range(SUP):
            part = pl.ds(t * TILE, TILE)
            for j in range(tile_cols):
                span = pl.ds(j * TILE, TILE)
                ref = masked_of(g)
                ref[part, span] = mask_tile(ref[part, span], listed[g * SUP + t, j])

    for i in range(pieces):
        relay(0, i)
    for q in range(aux_count):
        coef_copy(q).wait()
    for g in range(groups):
        await_far(g)
        work = list(lead_work(g))
        if g + 1 < groups:
            for i in range(pieces):
                relay(g + 1, i)
                if i < len(work):
                    work[i]()
            work = work[pieces:]
        for step in work:
            step()
        if g + 1 == groups:
            for e in range(groups):
                dens_copy(e).wait()
                mask_rows(e)
        await_last(g)
        for step in trail_work(g):
            step()

    for phase, u in [(p, u) for p in range(4) for u in range(units)]:
        if phase == 0:
            for h in range(2):
                stage_1(u, h).wait_recv()
                send_2[u, h] = (
                    partial[rows_of(u, h), columns_of(near[1 - h])]
                    + recv_1[u, h, 1].astype(jnp.float32)
                ).astype(jnp.bfloat16)
                stage_2(u, h).start()
        if phase == 1:
            ref, v = fock_of(u)
            for h in range(2):
                stage_2(u, h).wait_recv()
                total = (
                    partial[rows_of(u, h), columns_of(me)]
                    + recv_1[u, h, 0].astype(jnp.float32)
                    + recv_2[u, h].astype(jnp.float32)
                ) * scale
                diag[rows_of(u, h)] = total
                ref[rows_of(v, h), columns_of(me)] = total.astype(jnp.bfloat16)
            for axis in range(2):
                gather_1(u, axis).start()
        if phase == 2:
            for axis in range(2):
                gather_1(u, 1 - axis).wait_recv()
                gather_2(u, axis).start()
        if phase == 3:
            for axis in range(2):
                gather_2(u, axis).wait_recv()
            g = u // per_group
            if u % per_group == per_group - 1 and g < groups - 1:
                apply_rows(fock.at[pl.ds(g * W, W)], masked.at[g], early, g * W)
    for g in range(groups):
        for i in range(pieces):
            for p in range(2):
                @pl.when(sends(g, p, i) | is_owner)
                def _():
                    piece(g, p, i).wait_send()
                if direct(g, i):
                    pl.when(is_owner)(twin(g, p, i).wait_send)
    for u in range(units):
        for h in range(2):
            stage_1(u, h).wait_send()
            stage_2(u, h).wait_send()
            gather_1(u, h).wait_send()
            gather_2(u, h).wait_send()


def apply_rows(fock, masked, out, start, after=None):
    for j in range(masked.shape[1] // BAND):
        span = pl.ds(j * BAND, BAND)
        product = jnp.dot(fock[...], masked[:, span], preferred_element_type=jnp.float32)
        out[pl.ds(start, W), span] = (product * W ** (-0.5)).astype(jnp.bfloat16)
        if after is not None:
            after(j)


def apply_kernel(early, masked, fock, diag, result, diag_out, out, early_sem, out_sem, diag_sem):
    ready = early.shape[0]
    early_copy = pltpu.make_async_copy(early, result.at[pl.ds(0, ready)], early_sem)
    diag_copy = pltpu.make_async_copy(diag, diag_out, diag_sem)

    def out_copy(j):
        span = pl.ds(j * BAND, BAND)
        return pltpu.make_async_copy(
            out.at[:, span], result.at[pl.ds(ready, W), span], out_sem.at[j]
        )

    early_copy.start()
    diag_copy.start()
    apply_rows(fock, masked, out, 0, lambda j: out_copy(j).start())
    for j in range(masked.shape[1] // BAND):
        out_copy(j).wait()
    early_copy.wait()
    diag_copy.wait()


def per_device_whole(density, listed, three_centre):
    rows, cols = density.shape
    groups = rows // W
    units = rows // UNIT
    aux_count = three_centre.shape[0]
    aux_group = aux_count * lax.axis_size("col") // groups
    bf16, dma = jnp.bfloat16, pltpu.SemaphoreType.DMA
    in_hbm = pl.BlockSpec(memory_space=pltpu.HBM)
    in_vmem = pl.BlockSpec(memory_space=pltpu.VMEM)
    handed = pl.pallas_call(
        functools.partial(exchange_kernel, aux_group ** (-0.5)),
        out_shape=(
            pltpu.VMEM((rows - W, cols), bf16),
            pltpu.VMEM((W, cols), bf16),
            pltpu.VMEM((W, W), bf16),
            pltpu.VMEM((rows, TILE), jnp.float32),
        ),
        in_specs=[pl.BlockSpec(memory_space=pltpu.SMEM), in_hbm, in_hbm],
        out_specs=(in_vmem,) * 4,
        scratch_shapes=[
            pltpu.VMEM((groups, 2, W, HALF), bf16),
            pltpu.VMEM((groups, 2, W, HALF), bf16),
            pltpu.VMEM((aux_count, W, W), bf16),
            pltpu.VMEM((aux_count // groups, W, HALF), bf16),
            pltpu.VMEM((rows, W), jnp.float32),
            pltpu.VMEM((units, 2, 2, PART, TILE), bf16),
            pltpu.VMEM((units, 2, 2, PART, TILE), bf16),
            pltpu.VMEM((units, 2, PART, TILE), bf16),
            pltpu.VMEM((units, 2, PART, TILE), bf16),
            pltpu.VMEM((rows - W, W), bf16),
            pltpu.VMEM((groups - 1, W, cols), bf16),
            dma((groups, 2)),
            dma((aux_count,)),
            dma((groups,)),
            dma((groups, 2, W // PIECE)),
            dma((groups, 2, W // PIECE)),
            dma((groups, 2, W // PIECE)),
        ]
        + [dma((units, 2)) for _ in range(8)],
        compiler_params=pltpu.CompilerParams(
            collective_id=0, has_side_effects=True, vmem_limit_bytes=VMEM_GRANT
        ),
    )(*(pltpu.with_memory_space_constraint(value, pltpu.HBM) for value in (listed, density, three_centre)))
    result, diag = pl.pallas_call(
        apply_kernel,
        out_shape=(
            jax.ShapeDtypeStruct((rows, cols), bf16),
            jax.ShapeDtypeStruct((rows, TILE), jnp.float32),
        ),
        in_specs=[in_vmem] * 4,
        out_specs=(in_hbm, in_hbm),
        scratch_shapes=[pltpu.VMEM((W, cols), bf16), dma, dma((cols // BAND,)), dma],
        compiler_params=pltpu.CompilerParams(vmem_limit_bytes=VMEM_GRANT),
    )(*(pltpu.with_memory_space_constraint(value, pltpu.VMEM) for value in handed))
    return diag, result


def takes_whole(mesh, density, listed, three_centre):
    row_count, col_count = mesh.shape["row"], mesh.shape["col"]
    rows = density.shape[0] // row_count
    cols = density.shape[1] // col_count
    aux_count = three_centre.shape[0] // (row_count * col_count)
    if rows % W or rows < 2 * W or cols % rows or col_count != 4 or col_count * TILE != W:
        return False
    return aux_count % (rows // W) == 0


def solution(mesh):
    placed = (P("row", "col"), P("row", "col"), P(("row", "col"), None, None))

    def mapped(body):
        return jax.shard_map(
            body,
            mesh=mesh,
            in_specs=placed,
            out_specs=(P("row", "col"), P("row", "col")),
            check_vma=False,
        )

    def run(density, listed, three_centre):
        whole = takes_whole(mesh, density, listed, three_centre)
        return mapped(per_device_whole if whole else per_device)(density, listed, three_centre)

    return run
```

```python
import functools

import jax
import jax.numpy as jnp
from jax import lax
from jax.experimental import pallas as pl
from jax.experimental.pallas import tpu as pltpu
from jax.sharding import PartitionSpec as P

TILE = 128
W = 512
SUP = W // TILE
UNIT = W // 2
STRIP = W // 2
PART = UNIT // 2
PIECE = 64
HALF = W // 2
DIRECT = 3
BAND = 512
VMEM_GRANT = 32 * 2**20
MESH = pl.DeviceIdType.MESH


def from_root(value, axis, root):
    mine = lax.axis_index(axis) == root
    return lax.psum(jnp.where(mine, value, jnp.zeros_like(value)), axis)


def partner_2(block, axis, stride):
    count = lax.axis_size(axis)
    route = []
    for low in range(count):
        high = low | 1 << stride
        if high != low and high < count:
            route += [(low, high), (high, low)]
    return lax.ppermute(block, axis, route)


def halve_rows(values, row_index, levels, sender):
    for bit_level in reversed(range(levels)):
        middle = values.shape[0] // 2
        lower_half = row_index // 2**bit_level % 2 == 0
        kept_rows = jnp.where(lower_half, values[:middle], values[middle:])
        sent_rows = jnp.where(lower_half, values[middle:], values[:middle])
        values = kept_rows + sender(sent_rows, bit_level)
    return values


def per_device(density, listed, three_centre):
    tile_rows = listed.shape[0]
    tile_cols = listed.shape[1]
    quad_tiles = max(tile_rows, 4)
    groups_dev = quad_tiles // 4
    aux_count = three_centre.shape[0]
    col_count = lax.axis_size("col")
    row_index = lax.axis_index("row")
    col_index = lax.axis_index("col")
    masked = (
        density.reshape(tile_rows, TILE, tile_cols, TILE)
        * listed[:, None, :, None].astype(jnp.bfloat16)
    ).reshape(tile_rows * TILE, tile_cols * TILE)
    quad_start = row_index * tile_rows // quad_tiles * quad_tiles
    col_offset = quad_start % tile_cols * TILE
    portion = lax.dynamic_slice_in_dim(masked, col_offset, quad_tiles * TILE, 1)
    diagonal = from_root(portion, "col", quad_start // tile_cols)
    joined = jnp.concatenate([diagonal, masked], axis=1)
    levels = (quad_tiles // tile_rows).bit_length() - 1
    for bit_level in range(levels):
        partner = partner_2(joined, "row", bit_level)
        lower_half = row_index // 2**bit_level % 2 == 0
        joined = jnp.where(
            lower_half,
            jnp.concatenate([joined, partner], axis=0),
            jnp.concatenate([partner, joined], axis=0),
        )
    quad_block = joined[:, : quad_tiles * TILE]
    quad_density = joined[:, quad_tiles * TILE :]
    group_ids = jnp.arange(groups_dev, dtype=jnp.int32)
    exchange_quad = jnp.zeros((groups_dev, W, W), jnp.float32)
    for aux_slot in range(aux_count):
        group_slot = (col_index * aux_count + aux_slot) % groups_dev
        density_sub = lax.dynamic_slice(quad_block, (group_slot * W, group_slot * W), (W, W))
        aux_block = three_centre[aux_slot]
        half_product = jnp.dot(aux_block, density_sub, preferred_element_type=jnp.float32).astype(
            jnp.bfloat16
        )
        contribution = lax.dot_general(
            half_product, aux_block, (((1,), (1,)), ((), ())), preferred_element_type=jnp.float32
        )
        exchange_quad = exchange_quad + jnp.where(
            (group_ids == group_slot)[:, None, None], contribution[None], 0.0
        )
    aux_group = aux_count * col_count * 4 // tile_rows
    exchange_quad = (exchange_quad * aux_group ** (-0.5)).reshape(quad_tiles * TILE, W)
    column_share = lax.psum_scatter(exchange_quad, "col", scatter_dimension=1, tiled=True)
    exchange_diag = halve_rows(
        column_share,
        row_index,
        levels,
        lambda sent_rows, bit_level: partner_2(sent_rows, "row", bit_level),
    )
    fock_rounded = lax.all_gather(exchange_diag.astype(jnp.bfloat16), "col", axis=1, tiled=True)
    rows_here = tile_rows * TILE
    segment_rows = min(rows_here, W)
    segment_count = rows_here // segment_rows
    within_quad = (row_index * tile_rows - quad_start) * TILE
    products = []
    for segment in range(segment_count):
        group_position = (within_quad + segment * segment_rows) // W
        dens_rows = lax.dynamic_slice_in_dim(quad_density, group_position * W, W, 0)
        fock_part = fock_rounded[segment * segment_rows : (segment + 1) * segment_rows]
        products.append(
            jnp.dot(fock_part, dens_rows, preferred_element_type=jnp.float32) * W ** (-0.5)
        )
    exchange_density = jnp.concatenate(products, axis=0).astype(jnp.bfloat16)
    return (exchange_diag, exchange_density)


def mask_tile(tile, flag):
    return tile * jnp.full(tile.shape, flag.astype(jnp.float32)).astype(jnp.bfloat16)


def exchange_kernel(
    scale, listed, density, three_centre, early, masked_last, fock_last, diag,
    raw, block, coef, half, partial, send_1, recv_1, send_2, recv_2, fock, masked,
    raw_sem, coef_sem, dens_sem, bc_send, bc_recv, twin_send, rs1_send, rs1_recv,
    rs2_send, rs2_recv, ag1_send, ag1_recv, ag2_send, ag2_recv,
):
    tile_rows, tile_cols = listed.shape
    groups = tile_rows // SUP
    per_group = W // UNIT
    units = groups * per_group
    aux_count = three_centre.shape[0]
    row = lax.axis_index("row")
    me = lax.axis_index("col")
    x, y = me % 2, me // 2
    xn, yn = me + 1 - 2 * x, me + 2 - 4 * y
    far = xn + yn - me
    near = (xn, yn)
    first_tile = row * tile_rows
    owner = first_tile // tile_cols
    tile_off = first_tile % tile_cols
    ox, oy = owner % 2, owner // 2
    rx, ry = (x + ox) % 2, (y + oy) % 2
    even = (rx + ry + 1) % 2
    is_owner = rx + ry == 0
    is_far = rx + ry == 2
    hop_to = (xn * even + yn * (1 - even), yn * even + xn * (1 - even))
    last_of = (rx + 2 * (1 - ry) == 0, ry + 2 * (1 - rx) == 0)
    relays_of = (
        (rx + ry) * (rx + 1 - ry) > 0,
        (rx + ry) * (ry + 1 - rx) > 0,
    )
    lead = ry * (1 - rx)

    def remote(src, dst, send_sem, recv_sem, target):
        return pltpu.make_async_remote_copy(
            src_ref=src, dst_ref=dst, send_sem=send_sem, recv_sem=recv_sem,
            device_id=(row, target), device_id_type=MESH,
        )

    def raw_copy(g, p):
        start = (tile_off + g * SUP) * TILE + p * HALF
        columns = pl.ds(pl.multiple_of(start, TILE), HALF)
        return pltpu.make_async_copy(
            density.at[pl.ds(g * W, W), columns], raw.at[g, p], raw_sem.at[g]
        )

    def filled(ref, sem):
        pltpu.make_async_copy(ref, ref, sem).wait()

    def sent(ref, sem):
        remote(ref, ref, sem, sem, near[0]).wait_send()

    coef_copy = pltpu.make_async_copy(three_centre, coef, coef_sem)

    def masked_of(g):
        return masked.at[g] if g < groups - 1 else masked_last

    def dens_copy(g):
        return pltpu.make_async_copy(
            density.at[pl.ds(g * W, W)], masked_of(g), dens_sem.at[g]
        )

    pieces = W // PIECE

    def piece(g, p, i):
        part = block.at[g, p, pl.ds(i * PIECE, PIECE)]
        return remote(part, part, bc_send.at[g], bc_recv.at[g, p, i], hop_to[p])

    def relayed(g):
        return pieces - (DIRECT if g == groups - 1 else 0)

    def direct(g, i):
        return i >= relayed(g)

    def twin(g, p, i):
        part = block.at[g, p, pl.ds(i * PIECE, PIECE)]
        return remote(part, part, twin_send.at[g], bc_recv.at[g, p, i], hop_to[1 - p])

    @pl.when(is_owner)
    def _():
        for g in range(groups):
            for p in range(2):
                raw_copy(g, p).start()

    barrier = pltpu.get_barrier_semaphore()
    for neighbour in near:
        pl.semaphore_signal(barrier, inc=1, device_id=(row, neighbour), device_id_type=MESH)
    coef_copy.start()
    for g in range(groups):
        dens_copy(g).start()
    pl.semaphore_wait(barrier, 2)

    @pl.when(is_owner)
    def _():
        for g in range(groups):
            filled(raw.at[g], raw_sem.at[g])
            for i in range(pieces):
                rows = pl.ds(i * PIECE, PIECE)
                for p in range(2):
                    for j in range(HALF // TILE):
                        cols = pl.ds(j * TILE, TILE)
                        tile_col = tile_off + g * SUP + p * (HALF // TILE) + j
                        flag = listed[g * SUP + i * PIECE // TILE, tile_col]
                        block[g, p, rows, cols] = mask_tile(raw[g, p, rows, cols], flag)
                    piece(g, p, i).start()
                if direct(g, i):
                    for p in range(2):
                        twin(g, p, i).start()

    def sends(g, p, i):
        if direct(g, i):
            return relays_of[p] & jnp.logical_not(is_far)
        return relays_of[p]

    def relay(g, i):
        for p in range(2):
            @pl.when(sends(g, p, i))
            def _():
                piece(g, p, i).wait_recv()
                piece(g, p, i).start()

    def await_far(g):
        @pl.when(is_far)
        def _():
            for i in range(pieces):
                if direct(g, i):
                    for p in range(2):
                        piece(g, p, i).wait_recv()

    def await_last(g):
        for p in range(2):
            @pl.when(last_of[p])
            def _():
                for i in range(pieces):
                    piece(g, p, i).wait_recv()

    def stage_1(u, h):
        return remote(send_1.at[u, h], recv_1.at[u, h], rs1_send, rs1_recv.at[u, h], near[h])

    def stage_2(u, h):
        return remote(
            send_2.at[u, h], recv_2.at[u, h], rs2_send, rs2_recv.at[u, h], near[1 - h]
        )

    def columns_of(dev):
        return pl.ds(pl.multiple_of(dev * TILE, TILE), TILE)

    def rows_of(u, h):
        return pl.ds(u * UNIT + h * PART, PART)

    def fock_of(u):
        if u < units - per_group:
            return fock, u
        return fock_last, u - (units - per_group)

    def gather_1(u, axis):
        ref, v = fock_of(u)
        part = ref.at[pl.ds(v * UNIT, UNIT), columns_of(me)]
        return remote(part, part, ag1_send, ag1_recv.at[u, axis], near[axis])

    def gather_2(u, axis):
        ref, v = fock_of(u)
        part = ref.at[rows_of(v, axis), columns_of(near[1 - axis])]
        return remote(part, part, ag2_send, ag2_recv.at[u // per_group], near[axis])

    def members(g):
        return list(range(g, aux_count, groups))

    def columns_half(p):
        return pl.ds(pl.multiple_of(p * HALF, HALF), HALF)

    def first_products(g, p):
        for n, q in enumerate(members(g)):
            yield lambda n=n, q=q: half.__setitem__(
                n, jnp.dot(coef[q], block[g, p], preferred_element_type=jnp.float32).astype(jnp.bfloat16)
            )

    def second_product(g, p, v, fresh):
        rows = pl.ds(v * STRIP, STRIP)
        total = None
        for n, q in enumerate(members(g)):
            term = lax.dot_general(
                half[n, rows], coef[q, :, columns_half(p)], (((1,), (1,)), ((), ())),
                preferred_element_type=jnp.float32,
            )
            total = term if total is None else total + term
        at = pl.ds(g * W + v * STRIP, STRIP)
        if fresh:
            partial[at] = total
        else:
            partial[at] += total

    def send_unit(u):
        for h in range(2):
            send_1[u, h, 0] = partial[rows_of(u, h), columns_of(near[h])].astype(jnp.bfloat16)
            send_1[u, h, 1] = partial[rows_of(u, h), columns_of(far)].astype(jnp.bfloat16)
            stage_1(u, h).start()

    def lead_work(g):
        yield from first_products(g, lead)
        for v in range(W // STRIP):
            yield lambda v=v: second_product(g, lead, v, True)

    def trail_work(g):
        yield from first_products(g, 1 - lead)
        for v in range(W // STRIP):
            def step(v=v):
                second_product(g, 1 - lead, v, False)
                for u in range(v * STRIP // UNIT, (v + 1) * STRIP // UNIT):
                    send_unit(g * per_group + u)
            yield step

    def mask_rows(g):
        for t in range(SUP):
            part = pl.ds(t * TILE, TILE)
            for j in range(tile_cols):
                span = pl.ds(j * TILE, TILE)
                ref = masked_of(g)
                ref[part, span] = mask_tile(ref[part, span], listed[g * SUP + t, j])

    def mask_all():
        for g in range(groups):
            mask_rows(g)

    for i in range(pieces):
        relay(0, i)
    coef_copy.wait()
    for g in range(groups):
        await_far(g)
        work = list(lead_work(g))
        if g + 1 < groups:
            for i in range(pieces):
                relay(g + 1, i)
                if i < len(work):
                    work[i]()
            work = work[pieces:]
        for step in work:
            step()
        if g + 1 == groups:
            for e in range(groups):
                dens_copy(e).wait()
            pl.when(jnp.logical_not(is_far))(mask_all)
        await_last(g)
        for step in trail_work(g):
            step()
    pl.when(is_far)(mask_all)

    for phase, u in [(p, u) for p in range(4) for u in range(units)]:
        if phase == 0:
            for h in range(2):
                stage_1(u, h).wait_recv()
                send_2[u, h] = (
                    partial[rows_of(u, h), columns_of(near[1 - h])]
                    + recv_1[u, h, 1].astype(jnp.float32)
                ).astype(jnp.bfloat16)
                stage_2(u, h).start()
        if phase == 1:
            ref, v = fock_of(u)
            for h in range(2):
                stage_2(u, h).wait_recv()
                total = (
                    partial[rows_of(u, h), columns_of(me)]
                    + recv_1[u, h, 0].astype(jnp.float32)
                    + recv_2[u, h].astype(jnp.float32)
                ) * scale
                diag[rows_of(u, h)] = total
                ref[rows_of(v, h), columns_of(me)] = total.astype(jnp.bfloat16)
            for axis in range(2):
                gather_1(u, axis).start()
        if phase == 2:
            for axis in range(2):
                gather_1(u, 1 - axis).wait_recv()
                gather_2(u, axis).start()
        if phase == 3:
            g = u // per_group
            if u % per_group < per_group - 1:
                continue
            whole = masked_of(g).at[:, pl.ds(0, TILE)]
            remote(whole, whole, ag2_send, ag2_recv.at[g], near[0]).wait_recv()
            if g < groups - 1:
                apply_rows(fock.at[pl.ds(g * W, W)], masked.at[g], early, g * W)
    for g in range(groups):
        @pl.when(is_owner)
        def _():
            sent(block.at[g], bc_send.at[g])
            if relayed(g) < pieces:
                tail = pl.ds(relayed(g) * PIECE, W - relayed(g) * PIECE)
                sent(block.at[g, :, tail], twin_send.at[g])

        @pl.when(is_far)
        def _():
            sent(block.at[g, :, pl.ds(0, relayed(g) * PIECE)], bc_send.at[g])

        @pl.when(rx + ry == 1)
        def _():
            sent(block.at[g, 0], bc_send.at[g])
    sent(send_1, rs1_send)
    sent(send_2, rs2_send)
    sent(send_1, ag1_send)
    sent(send_1.at[:, 0], ag2_send)


def apply_rows(fock, masked, out, start, after=None):
    for j in range(masked.shape[1] // BAND):
        span = pl.ds(j * BAND, BAND)
        product = jnp.dot(fock[...], masked[:, span], preferred_element_type=jnp.float32)
        out[pl.ds(start, W), span] = (product * W ** (-0.5)).astype(jnp.bfloat16)
        if after is not None:
            after(j)


def apply_kernel(early, masked, fock, diag, result, diag_out, out, early_sem, out_sem, diag_sem):
    ready = early.shape[0]
    early_copy = pltpu.make_async_copy(early, result.at[pl.ds(0, ready)], early_sem)
    diag_copy = pltpu.make_async_copy(diag, diag_out, diag_sem)

    def out_copy(j):
        span = pl.ds(j * BAND, BAND)
        return pltpu.make_async_copy(
            out.at[:, span], result.at[pl.ds(ready, W), span], out_sem.at[j]
        )

    early_copy.start()
    diag_copy.start()
    apply_rows(fock, masked, out, 0, lambda j: out_copy(j).start())
    for j in range(masked.shape[1] // BAND):
        out_copy(j).wait()
    early_copy.wait()
    diag_copy.wait()


def per_device_whole(density, listed, three_centre):
    rows, cols = density.shape
    groups = rows // W
    units = rows // UNIT
    aux_count = three_centre.shape[0]
    aux_group = aux_count * lax.axis_size("col") // groups
    bf16, dma = jnp.bfloat16, pltpu.SemaphoreType.DMA
    in_hbm = pl.BlockSpec(memory_space=pltpu.HBM)
    in_vmem = pl.BlockSpec(memory_space=pltpu.VMEM)
    handed = pl.pallas_call(
        functools.partial(exchange_kernel, aux_group ** (-0.5)),
        out_shape=(
            pltpu.VMEM((rows - W, cols), bf16),
            pltpu.VMEM((W, cols), bf16),
            pltpu.VMEM((W, W), bf16),
            pltpu.VMEM((rows, TILE), jnp.float32),
        ),
        in_specs=[pl.BlockSpec(memory_space=pltpu.SMEM), in_hbm, in_hbm],
        out_specs=(in_vmem,) * 4,
        scratch_shapes=[
            pltpu.VMEM((groups, 2, W, HALF), bf16),
            pltpu.VMEM((groups, 2, W, HALF), bf16),
            pltpu.VMEM((aux_count, W, W), bf16),
            pltpu.VMEM((aux_count // groups, W, HALF), bf16),
            pltpu.VMEM((rows, W), jnp.float32),
            pltpu.VMEM((units, 2, 2, PART, TILE), bf16),
            pltpu.VMEM((units, 2, 2, PART, TILE), bf16),
            pltpu.VMEM((units, 2, PART, TILE), bf16),
            pltpu.VMEM((units, 2, PART, TILE), bf16),
            pltpu.VMEM((rows - W, W), bf16),
            pltpu.VMEM((groups - 1, W, cols), bf16),
            dma((groups,)),
            dma,
            dma((groups,)),
            dma((groups,)),
            dma((groups, 2, W // PIECE)),
            dma((groups,)),
            dma,
            dma((units, 2)),
            dma,
            dma((units, 2)),
            dma,
            dma((units, 2)),
            dma,
            dma((groups,)),
        ],
        compiler_params=pltpu.CompilerParams(
            collective_id=0, has_side_effects=True, vmem_limit_bytes=VMEM_GRANT
        ),
    )(*(pltpu.with_memory_space_constraint(value, pltpu.HBM) for value in (listed, density, three_centre)))
    result, diag = pl.pallas_call(
        apply_kernel,
        out_shape=(
            jax.ShapeDtypeStruct((rows, cols), bf16),
            jax.ShapeDtypeStruct((rows, TILE), jnp.float32),
        ),
        in_specs=[in_vmem] * 4,
        out_specs=(in_hbm, in_hbm),
        scratch_shapes=[pltpu.VMEM((W, cols), bf16), dma, dma((cols // BAND,)), dma],
        compiler_params=pltpu.CompilerParams(vmem_limit_bytes=VMEM_GRANT),
    )(*(pltpu.with_memory_space_constraint(value, pltpu.VMEM) for value in handed))
    return diag, result


def takes_whole(mesh, density, listed, three_centre):
    row_count, col_count = mesh.shape["row"], mesh.shape["col"]
    rows = density.shape[0] // row_count
    cols = density.shape[1] // col_count
    aux_count = three_centre.shape[0] // (row_count * col_count)
    if rows % W or rows < 2 * W or cols % rows or col_count != 4 or col_count * TILE != W:
        return False
    return aux_count % (rows // W) == 0


def solution(mesh):
    placed = (P("row", "col"), P("row", "col"), P(("row", "col"), None, None))

    def mapped(body):
        return jax.shard_map(
            body,
            mesh=mesh,
            in_specs=placed,
            out_specs=(P("row", "col"), P("row", "col")),
            check_vma=False,
        )

    def run(density, listed, three_centre):
        whole = takes_whole(mesh, density, listed, three_centre)
        return mapped(per_device_whole if whole else per_device)(density, listed, three_centre)

    return run
```

```python
import functools

import jax
import jax.numpy as jnp
from jax import lax
from jax.experimental import pallas as pl
from jax.experimental.pallas import tpu as pltpu
from jax.sharding import PartitionSpec as P

TILE = 128
W = 512
SUP = W // TILE
UNIT = W // 2
STRIP = W // 2
PART = UNIT // 2
PIECE = 64
HALF = W // 2
OFFSET_NS = 7000
DIRECT = 3
BAND = 512
VMEM_GRANT = 32 * 2**20
MESH = pl.DeviceIdType.MESH


def from_root(value, axis, root):
    mine = lax.axis_index(axis) == root
    return lax.psum(jnp.where(mine, value, jnp.zeros_like(value)), axis)


def partner_2(block, axis, stride):
    count = lax.axis_size(axis)
    route = []
    for low in range(count):
        high = low | 1 << stride
        if high != low and high < count:
            route += [(low, high), (high, low)]
    return lax.ppermute(block, axis, route)


def halve_rows(values, row_index, levels, sender):
    for bit_level in reversed(range(levels)):
        middle = values.shape[0] // 2
        lower_half = row_index // 2**bit_level % 2 == 0
        kept_rows = jnp.where(lower_half, values[:middle], values[middle:])
        sent_rows = jnp.where(lower_half, values[middle:], values[:middle])
        values = kept_rows + sender(sent_rows, bit_level)
    return values


def per_device(density, listed, three_centre):
    tile_rows = listed.shape[0]
    tile_cols = listed.shape[1]
    quad_tiles = max(tile_rows, 4)
    groups_dev = quad_tiles // 4
    aux_count = three_centre.shape[0]
    col_count = lax.axis_size("col")
    row_index = lax.axis_index("row")
    col_index = lax.axis_index("col")
    masked = (
        density.reshape(tile_rows, TILE, tile_cols, TILE)
        * listed[:, None, :, None].astype(jnp.bfloat16)
    ).reshape(tile_rows * TILE, tile_cols * TILE)
    quad_start = row_index * tile_rows // quad_tiles * quad_tiles
    col_offset = quad_start % tile_cols * TILE
    portion = lax.dynamic_slice_in_dim(masked, col_offset, quad_tiles * TILE, 1)
    diagonal = from_root(portion, "col", quad_start // tile_cols)
    joined = jnp.concatenate([diagonal, masked], axis=1)
    levels = (quad_tiles // tile_rows).bit_length() - 1
    for bit_level in range(levels):
        partner = partner_2(joined, "row", bit_level)
        lower_half = row_index // 2**bit_level % 2 == 0
        joined = jnp.where(
            lower_half,
            jnp.concatenate([joined, partner], axis=0),
            jnp.concatenate([partner, joined], axis=0),
        )
    quad_block = joined[:, : quad_tiles * TILE]
    quad_density = joined[:, quad_tiles * TILE :]
    group_ids = jnp.arange(groups_dev, dtype=jnp.int32)
    exchange_quad = jnp.zeros((groups_dev, W, W), jnp.float32)
    for aux_slot in range(aux_count):
        group_slot = (col_index * aux_count + aux_slot) % groups_dev
        density_sub = lax.dynamic_slice(quad_block, (group_slot * W, group_slot * W), (W, W))
        aux_block = three_centre[aux_slot]
        half_product = jnp.dot(aux_block, density_sub, preferred_element_type=jnp.float32).astype(
            jnp.bfloat16
        )
        contribution = lax.dot_general(
            half_product, aux_block, (((1,), (1,)), ((), ())), preferred_element_type=jnp.float32
        )
        exchange_quad = exchange_quad + jnp.where(
            (group_ids == group_slot)[:, None, None], contribution[None], 0.0
        )
    aux_group = aux_count * col_count * 4 // tile_rows
    exchange_quad = (exchange_quad * aux_group ** (-0.5)).reshape(quad_tiles * TILE, W)
    column_share = lax.psum_scatter(exchange_quad, "col", scatter_dimension=1, tiled=True)
    exchange_diag = halve_rows(
        column_share,
        row_index,
        levels,
        lambda sent_rows, bit_level: partner_2(sent_rows, "row", bit_level),
    )
    fock_rounded = lax.all_gather(exchange_diag.astype(jnp.bfloat16), "col", axis=1, tiled=True)
    rows_here = tile_rows * TILE
    segment_rows = min(rows_here, W)
    segment_count = rows_here // segment_rows
    within_quad = (row_index * tile_rows - quad_start) * TILE
    products = []
    for segment in range(segment_count):
        group_position = (within_quad + segment * segment_rows) // W
        dens_rows = lax.dynamic_slice_in_dim(quad_density, group_position * W, W, 0)
        fock_part = fock_rounded[segment * segment_rows : (segment + 1) * segment_rows]
        products.append(
            jnp.dot(fock_part, dens_rows, preferred_element_type=jnp.float32) * W ** (-0.5)
        )
    exchange_density = jnp.concatenate(products, axis=0).astype(jnp.bfloat16)
    return (exchange_diag, exchange_density)


def mask_tile(tile, flag):
    return tile * jnp.full(tile.shape, flag.astype(jnp.float32)).astype(jnp.bfloat16)


def exchange_kernel(
    scale, listed, density, three_centre, early, masked_last, fock_last, diag,
    raw, block, coef, half, partial, send_1, recv_1, send_2, recv_2, fock, masked,
    raw_sem, coef_sem, dens_sem, bc_send, bc_recv, twin_send, rs1_send, rs1_recv,
    rs2_send, rs2_recv, ag1_send, ag1_recv, ag2_send, ag2_recv,
):
    tile_rows, tile_cols = listed.shape
    groups = tile_rows // SUP
    per_group = W // UNIT
    units = groups * per_group
    aux_count = three_centre.shape[0]
    row = lax.axis_index("row")
    me = lax.axis_index("col")
    x, y = me % 2, me // 2
    xn, yn = me + 1 - 2 * x, me + 2 - 4 * y
    far = xn + yn - me
    near = (xn, yn)
    first_tile = row * tile_rows
    owner = first_tile // tile_cols
    tile_off = first_tile % tile_cols
    ox, oy = owner % 2, owner // 2
    rx, ry = (x + ox) % 2, (y + oy) % 2
    even = (rx + ry + 1) % 2
    is_owner = rx + ry == 0
    is_far = rx + ry == 2
    hop_to = (xn * even + yn * (1 - even), yn * even + xn * (1 - even))
    last_of = (rx + 2 * (1 - ry) == 0, ry + 2 * (1 - rx) == 0)
    relays_of = (
        (rx + ry) * (rx + 1 - ry) > 0,
        (rx + ry) * (ry + 1 - rx) > 0,
    )
    lead = ry * (1 - rx)

    def remote(src, dst, send_sem, recv_sem, target):
        return pltpu.make_async_remote_copy(
            src_ref=src, dst_ref=dst, send_sem=send_sem, recv_sem=recv_sem,
            device_id=(row, target), device_id_type=MESH,
        )

    def raw_copy(g, p):
        start = (tile_off + g * SUP) * TILE + p * HALF
        columns = pl.ds(pl.multiple_of(start, TILE), HALF)
        return pltpu.make_async_copy(
            density.at[pl.ds(g * W, W), columns], raw.at[g, p], raw_sem.at[g]
        )

    def filled(ref, sem):
        pltpu.make_async_copy(ref, ref, sem).wait()

    def sent(ref, sem):
        remote(ref, ref, sem, sem, near[0]).wait_send()

    coef_copy = pltpu.make_async_copy(three_centre, coef, coef_sem)

    def masked_of(g):
        return masked.at[g] if g < groups - 1 else masked_last

    def dens_copy(g):
        return pltpu.make_async_copy(
            density.at[pl.ds(g * W, W)], masked_of(g), dens_sem.at[g]
        )

    pieces = W // PIECE

    def piece(g, p, i):
        part = block.at[g, p, pl.ds(i * PIECE, PIECE)]
        return remote(part, part, bc_send.at[g], bc_recv.at[g, p, i], hop_to[p])

    def relayed(g):
        return pieces - (DIRECT if g == groups - 1 else 0)

    def direct(g, i):
        return i >= relayed(g)

    def twin(g, p, i):
        part = block.at[g, p, pl.ds(i * PIECE, PIECE)]
        return remote(part, part, twin_send.at[g], bc_recv.at[g, p, i], hop_to[1 - p])

    barrier = pltpu.get_barrier_semaphore()
    for neighbour in near:
        pl.semaphore_signal(barrier, inc=1, device_id=(row, neighbour), device_id_type=MESH)

    @pl.when(is_owner)
    def _():
        for g in range(groups):
            for p in range(2):
                raw_copy(g, p).start()

    pl.semaphore_wait(barrier, 2)

    @pl.when(is_owner)
    def _():
        for g in range(groups):
            filled(raw.at[g], raw_sem.at[g])
            if g == groups - 1:
                @pl.when(row % 2 == 1)
                def _():
                    pl.delay(OFFSET_NS)
            for i in range(pieces):
                rows = pl.ds(i * PIECE, PIECE)
                for p in range(2):
                    for j in range(HALF // TILE):
                        cols = pl.ds(j * TILE, TILE)
                        tile_col = tile_off + g * SUP + p * (HALF // TILE) + j
                        flag = listed[g * SUP + i * PIECE // TILE, tile_col]
                        block[g, p, rows, cols] = mask_tile(raw[g, p, rows, cols], flag)
                    piece(g, p, i).start()
                if direct(g, i):
                    for p in range(2):
                        twin(g, p, i).start()

    def sends(g, p, i):
        if direct(g, i):
            return relays_of[p] & jnp.logical_not(is_far)
        return relays_of[p]

    def relay(g, i):
        for p in range(2):
            @pl.when(sends(g, p, i))
            def _():
                piece(g, p, i).wait_recv()
                piece(g, p, i).start()

    def await_far(g):
        @pl.when(is_far)
        def _():
            for i in range(pieces):
                if direct(g, i):
                    for p in range(2):
                        piece(g, p, i).wait_recv()

    def await_last(g):
        for p in range(2):
            @pl.when(last_of[p])
            def _():
                for i in range(pieces):
                    piece(g, p, i).wait_recv()

    def stage_1(u, h):
        return remote(send_1.at[u, h], recv_1.at[u, h], rs1_send, rs1_recv.at[u, h], near[h])

    def stage_2(u, h):
        return remote(
            send_2.at[u, h], recv_2.at[u, h], rs2_send, rs2_recv.at[u, h], near[1 - h]
        )

    def columns_of(dev):
        return pl.ds(pl.multiple_of(dev * TILE, TILE), TILE)

    def rows_of(u, h):
        return pl.ds(u * UNIT + h * PART, PART)

    def fock_of(u):
        if u < units - per_group:
            return fock, u
        return fock_last, u - (units - per_group)

    def gather_1(u, axis):
        ref, v = fock_of(u)
        part = ref.at[pl.ds(v * UNIT, UNIT), columns_of(me)]
        return remote(part, part, ag1_send, ag1_recv.at[u, axis], near[axis])

    def gather_2(u, axis):
        ref, v = fock_of(u)
        part = ref.at[rows_of(v, axis), columns_of(near[1 - axis])]
        return remote(part, part, ag2_send, ag2_recv.at[u // per_group], near[axis])

    def members(g):
        return list(range(g, aux_count, groups))

    def columns_half(p):
        return pl.ds(pl.multiple_of(p * HALF, HALF), HALF)

    def first_products(g, p):
        for n, q in enumerate(members(g)):
            yield lambda n=n, q=q: half.__setitem__(
                n, jnp.dot(coef[q], block[g, p], preferred_element_type=jnp.float32).astype(jnp.bfloat16)
            )

    def second_product(g, p, v, fresh):
        rows = pl.ds(v * STRIP, STRIP)
        total = None
        for n, q in enumerate(members(g)):
            term = lax.dot_general(
                half[n, rows], coef[q, :, columns_half(p)], (((1,), (1,)), ((), ())),
                preferred_element_type=jnp.float32,
            )
            total = term if total is None else total + term
        at = pl.ds(g * W + v * STRIP, STRIP)
        if fresh:
            partial[at] = total
        else:
            partial[at] += total

    def send_unit(u):
        for h in range(2):
            send_1[u, h, 0] = partial[rows_of(u, h), columns_of(near[h])].astype(jnp.bfloat16)
            send_1[u, h, 1] = partial[rows_of(u, h), columns_of(far)].astype(jnp.bfloat16)
            stage_1(u, h).start()

    def lead_work(g):
        yield from first_products(g, lead)
        for v in range(W // STRIP):
            yield lambda v=v: second_product(g, lead, v, True)

    def trail_work(g):
        yield from first_products(g, 1 - lead)
        for v in range(W // STRIP):
            def step(v=v):
                second_product(g, 1 - lead, v, False)
                for u in range(v * STRIP // UNIT, (v + 1) * STRIP // UNIT):
                    send_unit(g * per_group + u)
            yield step

    def mask_rows(g):
        for t in range(SUP):
            part = pl.ds(t * TILE, TILE)
            for j in range(tile_cols):
                span = pl.ds(j * TILE, TILE)
                ref = masked_of(g)
                ref[part, span] = mask_tile(ref[part, span], listed[g * SUP + t, j])

    def mask_all():
        for g in range(groups):
            mask_rows(g)

    coef_copy.start()
    for g in range(groups):
        dens_copy(g).start()
    for i in range(pieces):
        relay(0, i)
    coef_copy.wait()
    for g in range(groups):
        await_far(g)
        work = list(lead_work(g))
        if g + 1 < groups:
            for i in range(pieces):
                relay(g + 1, i)
                if i < len(work):
                    work[i]()
            work = work[pieces:]
        for step in work:
            step()
        if g + 1 == groups:
            for e in range(groups):
                dens_copy(e).wait()
            pl.when(jnp.logical_not(is_far))(mask_all)
        await_last(g)
        for step in trail_work(g):
            step()
    pl.when(is_far)(mask_all)

    for phase, u in [(p, u) for p in range(4) for u in range(units)]:
        if phase == 0:
            for h in range(2):
                stage_1(u, h).wait_recv()
                send_2[u, h] = (
                    partial[rows_of(u, h), columns_of(near[1 - h])]
                    + recv_1[u, h, 1].astype(jnp.float32)
                ).astype(jnp.bfloat16)
                stage_2(u, h).start()
        if phase == 1:
            ref, v = fock_of(u)
            for h in range(2):
                stage_2(u, h).wait_recv()
                total = (
                    partial[rows_of(u, h), columns_of(me)]
                    + recv_1[u, h, 0].astype(jnp.float32)
                    + recv_2[u, h].astype(jnp.float32)
                ) * scale
                diag[rows_of(u, h)] = total
                ref[rows_of(v, h), columns_of(me)] = total.astype(jnp.bfloat16)
            for axis in range(2):
                gather_1(u, axis).start()
        if phase == 2:
            for axis in range(2):
                gather_1(u, 1 - axis).wait_recv()
                gather_2(u, axis).start()
        if phase == 3:
            g = u // per_group
            if u % per_group < per_group - 1:
                continue
            whole = masked_of(g).at[:, pl.ds(0, TILE)]
            remote(whole, whole, ag2_send, ag2_recv.at[g], near[0]).wait_recv()
            if g < groups - 1:
                apply_rows(fock.at[pl.ds(g * W, W)], masked.at[g], early, g * W)
    for g in range(groups):
        @pl.when(is_owner)
        def _():
            sent(block.at[g], bc_send.at[g])
            if relayed(g) < pieces:
                tail = pl.ds(relayed(g) * PIECE, W - relayed(g) * PIECE)
                sent(block.at[g, :, tail], twin_send.at[g])

        @pl.when(is_far)
        def _():
            sent(block.at[g, :, pl.ds(0, relayed(g) * PIECE)], bc_send.at[g])

        @pl.when(rx + ry == 1)
        def _():
            sent(block.at[g, 0], bc_send.at[g])
    sent(send_1, rs1_send)
    sent(send_2, rs2_send)
    sent(send_1, ag1_send)
    sent(send_1.at[:, 0], ag2_send)


def apply_rows(fock, masked, out, start, after=None):
    for j in range(masked.shape[1] // BAND):
        span = pl.ds(j * BAND, BAND)
        product = jnp.dot(fock[...], masked[:, span], preferred_element_type=jnp.float32)
        out[pl.ds(start, W), span] = (product * W ** (-0.5)).astype(jnp.bfloat16)
        if after is not None:
            after(j)


def apply_kernel(early, masked, fock, diag, result, diag_out, out, early_sem, out_sem, diag_sem):
    ready = early.shape[0]
    early_copy = pltpu.make_async_copy(early, result.at[pl.ds(0, ready)], early_sem)
    diag_copy = pltpu.make_async_copy(diag, diag_out, diag_sem)

    def out_copy(j):
        span = pl.ds(j * BAND, BAND)
        return pltpu.make_async_copy(
            out.at[:, span], result.at[pl.ds(ready, W), span], out_sem.at[j]
        )

    early_copy.start()
    diag_copy.start()
    apply_rows(fock, masked, out, 0, lambda j: out_copy(j).start())
    for j in range(masked.shape[1] // BAND):
        out_copy(j).wait()
    early_copy.wait()
    diag_copy.wait()


def per_device_whole(density, listed, three_centre):
    rows, cols = density.shape
    groups = rows // W
    units = rows // UNIT
    aux_count = three_centre.shape[0]
    aux_group = aux_count * lax.axis_size("col") // groups
    bf16, dma = jnp.bfloat16, pltpu.SemaphoreType.DMA
    in_hbm = pl.BlockSpec(memory_space=pltpu.HBM)
    in_vmem = pl.BlockSpec(memory_space=pltpu.VMEM)
    handed = pl.pallas_call(
        functools.partial(exchange_kernel, aux_group ** (-0.5)),
        out_shape=(
            pltpu.VMEM((rows - W, cols), bf16),
            pltpu.VMEM((W, cols), bf16),
            pltpu.VMEM((W, W), bf16),
            pltpu.VMEM((rows, TILE), jnp.float32),
        ),
        in_specs=[pl.BlockSpec(memory_space=pltpu.SMEM), in_hbm, in_hbm],
        out_specs=(in_vmem,) * 4,
        scratch_shapes=[
            pltpu.VMEM((groups, 2, W, HALF), bf16),
            pltpu.VMEM((groups, 2, W, HALF), bf16),
            pltpu.VMEM((aux_count, W, W), bf16),
            pltpu.VMEM((aux_count // groups, W, HALF), bf16),
            pltpu.VMEM((rows, W), jnp.float32),
            pltpu.VMEM((units, 2, 2, PART, TILE), bf16),
            pltpu.VMEM((units, 2, 2, PART, TILE), bf16),
            pltpu.VMEM((units, 2, PART, TILE), bf16),
            pltpu.VMEM((units, 2, PART, TILE), bf16),
            pltpu.VMEM((rows - W, W), bf16),
            pltpu.VMEM((groups - 1, W, cols), bf16),
            dma((groups,)),
            dma,
            dma((groups,)),
            dma((groups,)),
            dma((groups, 2, W // PIECE)),
            dma((groups,)),
            dma,
            dma((units, 2)),
            dma,
            dma((units, 2)),
            dma,
            dma((units, 2)),
            dma,
            dma((groups,)),
        ],
        compiler_params=pltpu.CompilerParams(
            collective_id=0, has_side_effects=True, vmem_limit_bytes=VMEM_GRANT
        ),
    )(*(pltpu.with_memory_space_constraint(value, pltpu.HBM) for value in (listed, density, three_centre)))
    result, diag = pl.pallas_call(
        apply_kernel,
        out_shape=(
            jax.ShapeDtypeStruct((rows, cols), bf16),
            jax.ShapeDtypeStruct((rows, TILE), jnp.float32),
        ),
        in_specs=[in_vmem] * 4,
        out_specs=(in_hbm, in_hbm),
        scratch_shapes=[pltpu.VMEM((W, cols), bf16), dma, dma((cols // BAND,)), dma],
        compiler_params=pltpu.CompilerParams(vmem_limit_bytes=VMEM_GRANT),
    )(*(pltpu.with_memory_space_constraint(value, pltpu.VMEM) for value in handed))
    return diag, result


def takes_whole(mesh, density, listed, three_centre):
    row_count, col_count = mesh.shape["row"], mesh.shape["col"]
    rows = density.shape[0] // row_count
    cols = density.shape[1] // col_count
    aux_count = three_centre.shape[0] // (row_count * col_count)
    if rows % W or rows < 2 * W or cols % rows or col_count != 4 or col_count * TILE != W:
        return False
    return aux_count % (rows // W) == 0


def solution(mesh):
    placed = (P("row", "col"), P("row", "col"), P(("row", "col"), None, None))

    def mapped(body):
        return jax.shard_map(
            body,
            mesh=mesh,
            in_specs=placed,
            out_specs=(P("row", "col"), P("row", "col")),
            check_vma=False,
        )

    def run(density, listed, three_centre):
        whole = takes_whole(mesh, density, listed, three_centre)
        return mapped(per_device_whole if whole else per_device)(density, listed, three_centre)

    return run
```

```python
import functools

import jax
import jax.numpy as jnp
from jax import lax
from jax.experimental import pallas as pl
from jax.experimental.pallas import tpu as pltpu
from jax.sharding import PartitionSpec as P

TILE = 128
W = 512
SUP = W // TILE
UNIT = W // 2
STRIP = W // 2
PART = UNIT // 2
PIECE = 64
HALF = W // 2
OFFSET_NS = 7000
DIRECT = 3
BAND = 512
VMEM_GRANT = 32 * 2**20
MESH = pl.DeviceIdType.MESH


def from_root(value, axis, root):
    mine = lax.axis_index(axis) == root
    return lax.psum(jnp.where(mine, value, jnp.zeros_like(value)), axis)


def partner_2(block, axis, stride):
    count = lax.axis_size(axis)
    route = []
    for low in range(count):
        high = low | 1 << stride
        if high != low and high < count:
            route += [(low, high), (high, low)]
    return lax.ppermute(block, axis, route)


def halve_rows(values, row_index, levels, sender):
    for bit_level in reversed(range(levels)):
        middle = values.shape[0] // 2
        lower_half = row_index // 2**bit_level % 2 == 0
        kept_rows = jnp.where(lower_half, values[:middle], values[middle:])
        sent_rows = jnp.where(lower_half, values[middle:], values[:middle])
        values = kept_rows + sender(sent_rows, bit_level)
    return values


def per_device(density, listed, three_centre):
    tile_rows = listed.shape[0]
    tile_cols = listed.shape[1]
    quad_tiles = max(tile_rows, 4)
    groups_dev = quad_tiles // 4
    aux_count = three_centre.shape[0]
    col_count = lax.axis_size("col")
    row_index = lax.axis_index("row")
    col_index = lax.axis_index("col")
    masked = (
        density.reshape(tile_rows, TILE, tile_cols, TILE)
        * listed[:, None, :, None].astype(jnp.bfloat16)
    ).reshape(tile_rows * TILE, tile_cols * TILE)
    quad_start = row_index * tile_rows // quad_tiles * quad_tiles
    col_offset = quad_start % tile_cols * TILE
    portion = lax.dynamic_slice_in_dim(masked, col_offset, quad_tiles * TILE, 1)
    diagonal = from_root(portion, "col", quad_start // tile_cols)
    joined = jnp.concatenate([diagonal, masked], axis=1)
    levels = (quad_tiles // tile_rows).bit_length() - 1
    for bit_level in range(levels):
        partner = partner_2(joined, "row", bit_level)
        lower_half = row_index // 2**bit_level % 2 == 0
        joined = jnp.where(
            lower_half,
            jnp.concatenate([joined, partner], axis=0),
            jnp.concatenate([partner, joined], axis=0),
        )
    quad_block = joined[:, : quad_tiles * TILE]
    quad_density = joined[:, quad_tiles * TILE :]
    group_ids = jnp.arange(groups_dev, dtype=jnp.int32)
    exchange_quad = jnp.zeros((groups_dev, W, W), jnp.float32)
    for aux_slot in range(aux_count):
        group_slot = (col_index * aux_count + aux_slot) % groups_dev
        density_sub = lax.dynamic_slice(quad_block, (group_slot * W, group_slot * W), (W, W))
        aux_block = three_centre[aux_slot]
        half_product = jnp.dot(aux_block, density_sub, preferred_element_type=jnp.float32).astype(
            jnp.bfloat16
        )
        contribution = lax.dot_general(
            half_product, aux_block, (((1,), (1,)), ((), ())), preferred_element_type=jnp.float32
        )
        exchange_quad = exchange_quad + jnp.where(
            (group_ids == group_slot)[:, None, None], contribution[None], 0.0
        )
    aux_group = aux_count * col_count * 4 // tile_rows
    exchange_quad = (exchange_quad * aux_group ** (-0.5)).reshape(quad_tiles * TILE, W)
    column_share = lax.psum_scatter(exchange_quad, "col", scatter_dimension=1, tiled=True)
    exchange_diag = halve_rows(
        column_share,
        row_index,
        levels,
        lambda sent_rows, bit_level: partner_2(sent_rows, "row", bit_level),
    )
    fock_rounded = lax.all_gather(exchange_diag.astype(jnp.bfloat16), "col", axis=1, tiled=True)
    rows_here = tile_rows * TILE
    segment_rows = min(rows_here, W)
    segment_count = rows_here // segment_rows
    within_quad = (row_index * tile_rows - quad_start) * TILE
    products = []
    for segment in range(segment_count):
        group_position = (within_quad + segment * segment_rows) // W
        dens_rows = lax.dynamic_slice_in_dim(quad_density, group_position * W, W, 0)
        fock_part = fock_rounded[segment * segment_rows : (segment + 1) * segment_rows]
        products.append(
            jnp.dot(fock_part, dens_rows, preferred_element_type=jnp.float32) * W ** (-0.5)
        )
    exchange_density = jnp.concatenate(products, axis=0).astype(jnp.bfloat16)
    return (exchange_diag, exchange_density)


def mask_tile(tile, flag):
    return tile * jnp.full(tile.shape, flag.astype(jnp.float32)).astype(jnp.bfloat16)


def exchange_kernel(
    scale, listed, density, three_centre, early, masked_last, fock_last, diag,
    raw, block, coef, half, partial, send_1, recv_1, send_2, recv_2, fock, masked,
    raw_sem, coef_sem, dens_sem, bc_send, bc_recv, twin_send, rs1_send, rs1_recv,
    rs2_send, rs2_recv, ag1_send, ag1_recv, ag2_send, ag2_recv,
):
    tile_rows, tile_cols = listed.shape
    groups = tile_rows // SUP
    per_group = W // UNIT
    units = groups * per_group
    aux_count = three_centre.shape[0]
    row = lax.axis_index("row")
    me = lax.axis_index("col")
    x, y = me % 2, me // 2
    xn, yn = me + 1 - 2 * x, me + 2 - 4 * y
    far = xn + yn - me
    near = (xn, yn)
    first_tile = row * tile_rows
    owner = first_tile // tile_cols
    tile_off = first_tile % tile_cols
    ox, oy = owner % 2, owner // 2
    rx, ry = (x + ox) % 2, (y + oy) % 2
    even = (rx + ry + 1) % 2
    is_owner = rx + ry == 0
    is_far = rx + ry == 2
    hop_to = (xn * even + yn * (1 - even), yn * even + xn * (1 - even))
    last_of = (rx + 2 * (1 - ry) == 0, ry + 2 * (1 - rx) == 0)
    relays_of = (
        (rx + ry) * (rx + 1 - ry) > 0,
        (rx + ry) * (ry + 1 - rx) > 0,
    )
    lead = ry * (1 - rx)

    def remote(src, dst, send_sem, recv_sem, target):
        return pltpu.make_async_remote_copy(
            src_ref=src, dst_ref=dst, send_sem=send_sem, recv_sem=recv_sem,
            device_id=(row, target), device_id_type=MESH,
        )

    def raw_copy(g, p):
        start = (tile_off + g * SUP) * TILE + p * HALF
        columns = pl.ds(pl.multiple_of(start, TILE), HALF)
        return pltpu.make_async_copy(
            density.at[pl.ds(g * W, W), columns], raw.at[g, p], raw_sem.at[g]
        )

    def filled(ref, sem):
        pltpu.make_async_copy(ref, ref, sem).wait()

    def sent(ref, sem):
        remote(ref, ref, sem, sem, near[0]).wait_send()

    coef_copy = pltpu.make_async_copy(three_centre, coef, coef_sem)

    def masked_of(g):
        return masked.at[g] if g < groups - 1 else masked_last

    def dens_copy(g):
        return pltpu.make_async_copy(
            density.at[pl.ds(g * W, W)], masked_of(g), dens_sem.at[g]
        )

    pieces = W // PIECE

    def piece(g, p, i):
        part = block.at[g, p, pl.ds(i * PIECE, PIECE)]
        return remote(part, part, bc_send.at[g], bc_recv.at[g, p, i], hop_to[p])

    def relayed(g):
        return pieces - (DIRECT if g == groups - 1 else 0)

    def direct(g, i):
        return i >= relayed(g)

    def twin(g, p, i):
        part = block.at[g, p, pl.ds(i * PIECE, PIECE)]
        return remote(part, part, twin_send.at[g], bc_recv.at[g, p, i], hop_to[1 - p])

    barrier = pltpu.get_barrier_semaphore()
    for neighbour in near:
        pl.semaphore_signal(barrier, inc=1, device_id=(row, neighbour), device_id_type=MESH)

    @pl.when(is_owner)
    def _():
        for g in range(groups):
            for p in range(2):
                raw_copy(g, p).start()

    pl.semaphore_wait(barrier, 2)

    @pl.when(is_owner)
    def _():
        for g in range(groups):
            filled(raw.at[g], raw_sem.at[g])
            if g == groups - 1:
                @pl.when(row % 2 == 1)
                def _():
                    pl.delay(OFFSET_NS)
            for i in range(pieces):
                rows = pl.ds(i * PIECE, PIECE)
                for p in range(2):
                    for j in range(HALF // TILE):
                        cols = pl.ds(j * TILE, TILE)
                        tile_col = tile_off + g * SUP + p * (HALF // TILE) + j
                        flag = listed[g * SUP + i * PIECE // TILE, tile_col]
                        block[g, p, rows, cols] = mask_tile(raw[g, p, rows, cols], flag)
                    piece(g, p, i).start()
                if direct(g, i):
                    for p in range(2):
                        twin(g, p, i).start()

    def sends(g, p, i):
        if direct(g, i):
            return relays_of[p] & jnp.logical_not(is_far)
        return relays_of[p]

    def relay(g, i):
        for p in range(2):
            @pl.when(sends(g, p, i))
            def _():
                piece(g, p, i).wait_recv()
                piece(g, p, i).start()

    def await_far(g):
        @pl.when(is_far)
        def _():
            for i in range(pieces):
                if direct(g, i):
                    for p in range(2):
                        piece(g, p, i).wait_recv()

    def await_last(g):
        for p in range(2):
            @pl.when(last_of[p])
            def _():
                for i in range(pieces):
                    piece(g, p, i).wait_recv()

    def stage_1(u, h):
        return remote(send_1.at[u, h], recv_1.at[u, h], rs1_send, rs1_recv.at[u, h], near[h])

    def stage_2(u, h):
        return remote(
            send_2.at[u, h], recv_2.at[u, h], rs2_send, rs2_recv.at[u, h], near[1 - h]
        )

    def columns_of(dev):
        return pl.ds(pl.multiple_of(dev * TILE, TILE), TILE)

    def rows_of(u, h):
        return pl.ds(u * UNIT + h * PART, PART)

    def fock_of(u):
        if u < units - per_group:
            return fock, u
        return fock_last, u - (units - per_group)

    def gather_1(u, axis):
        ref, v = fock_of(u)
        part = ref.at[pl.ds(v * UNIT, UNIT), columns_of(me)]
        return remote(part, part, ag1_send, ag1_recv.at[u, axis], near[axis])

    def gather_2(u, axis):
        ref, v = fock_of(u)
        part = ref.at[rows_of(v, axis), columns_of(near[1 - axis])]
        return remote(part, part, ag2_send, ag2_recv.at[u // per_group], near[axis])

    def members(g):
        return list(range(g, aux_count, groups))

    def columns_half(p):
        return pl.ds(pl.multiple_of(p * HALF, HALF), HALF)

    def first_products(g, p):
        for n, q in enumerate(members(g)):
            yield lambda n=n, q=q: half.__setitem__(
                n, jnp.dot(coef[q], block[g, p], preferred_element_type=jnp.float32).astype(jnp.bfloat16)
            )

    def second_product(g, p, v, fresh):
        rows = pl.ds(v * STRIP, STRIP)
        total = None
        for n, q in enumerate(members(g)):
            term = lax.dot_general(
                half[n, rows], coef[q, :, columns_half(p)], (((1,), (1,)), ((), ())),
                preferred_element_type=jnp.float32,
            )
            total = term if total is None else total + term
        at = pl.ds(g * W + v * STRIP, STRIP)
        if fresh:
            partial[at] = total
        else:
            partial[at] += total

    def send_unit(u):
        for h in range(2):
            send_1[u, h, 0] = partial[rows_of(u, h), columns_of(near[h])].astype(jnp.bfloat16)
            send_1[u, h, 1] = partial[rows_of(u, h), columns_of(far)].astype(jnp.bfloat16)
            stage_1(u, h).start()

    def lead_work(g):
        yield from first_products(g, lead)
        for v in range(W // STRIP):
            yield lambda v=v: second_product(g, lead, v, True)

    def trail_work(g):
        for v in range(W // STRIP):
            def step(v=v):
                rows = pl.ds(v * STRIP, STRIP)
                for n, q in enumerate(members(g)):
                    half[n, rows] = jnp.dot(
                        coef[q, rows], block[g, 1 - lead], preferred_element_type=jnp.float32
                    ).astype(jnp.bfloat16)
                second_product(g, 1 - lead, v, False)
                for u in range(v * STRIP // UNIT, (v + 1) * STRIP // UNIT):
                    send_unit(g * per_group + u)
            yield step

    def mask_rows(g):
        for t in range(SUP):
            part = pl.ds(t * TILE, TILE)
            for j in range(tile_cols):
                span = pl.ds(j * TILE, TILE)
                ref = masked_of(g)
                ref[part, span] = mask_tile(ref[part, span], listed[g * SUP + t, j])

    def mask_all():
        for g in range(groups):
            mask_rows(g)

    coef_copy.start()
    for g in range(groups):
        dens_copy(g).start()
    for i in range(pieces):
        relay(0, i)
    coef_copy.wait()
    for g in range(groups):
        await_far(g)
        work = list(lead_work(g))
        if g + 1 < groups:
            for i in range(pieces):
                relay(g + 1, i)
                if i < len(work):
                    work[i]()
            work = work[pieces:]
        for step in work:
            step()
        if g + 1 == groups:
            for e in range(groups):
                dens_copy(e).wait()
            pl.when(jnp.logical_not(is_far))(mask_all)
        await_last(g)
        for step in trail_work(g):
            step()
    pl.when(is_far)(mask_all)

    for phase, u in [(p, u) for p in range(4) for u in range(units)]:
        if phase == 0:
            for h in range(2):
                stage_1(u, h).wait_recv()
                send_2[u, h] = (
                    partial[rows_of(u, h), columns_of(near[1 - h])]
                    + recv_1[u, h, 1].astype(jnp.float32)
                ).astype(jnp.bfloat16)
                stage_2(u, h).start()
        if phase == 1:
            ref, v = fock_of(u)
            for h in range(2):
                stage_2(u, h).wait_recv()
                total = (
                    partial[rows_of(u, h), columns_of(me)]
                    + recv_1[u, h, 0].astype(jnp.float32)
                    + recv_2[u, h].astype(jnp.float32)
                ) * scale
                diag[rows_of(u, h)] = total
                ref[rows_of(v, h), columns_of(me)] = total.astype(jnp.bfloat16)
            for axis in range(2):
                gather_1(u, axis).start()
        if phase == 2:
            for axis in range(2):
                gather_1(u, 1 - axis).wait_recv()
                gather_2(u, axis).start()
        if phase == 3:
            g = u // per_group
            if u % per_group < per_group - 1:
                continue
            whole = masked_of(g).at[:, pl.ds(0, TILE)]
            remote(whole, whole, ag2_send, ag2_recv.at[g], near[0]).wait_recv()
            if g < groups - 1:
                apply_rows(fock.at[pl.ds(g * W, W)], masked.at[g], early, g * W)
    for g in range(groups):
        @pl.when(is_owner)
        def _():
            sent(block.at[g], bc_send.at[g])
            if relayed(g) < pieces:
                tail = pl.ds(relayed(g) * PIECE, W - relayed(g) * PIECE)
                sent(block.at[g, :, tail], twin_send.at[g])

        @pl.when(is_far)
        def _():
            sent(block.at[g, :, pl.ds(0, relayed(g) * PIECE)], bc_send.at[g])

        @pl.when(rx + ry == 1)
        def _():
            sent(block.at[g, 0], bc_send.at[g])
    sent(send_1, rs1_send)
    sent(send_2, rs2_send)
    sent(send_1, ag1_send)
    sent(send_1.at[:, 0], ag2_send)


def apply_rows(fock, masked, out, start, after=None):
    for j in range(masked.shape[1] // BAND):
        span = pl.ds(j * BAND, BAND)
        product = jnp.dot(fock[...], masked[:, span], preferred_element_type=jnp.float32)
        out[pl.ds(start, W), span] = (product * W ** (-0.5)).astype(jnp.bfloat16)
        if after is not None:
            after(j)


def apply_kernel(early, masked, fock, diag, result, diag_out, out, early_sem, out_sem, diag_sem):
    ready = early.shape[0]
    early_copy = pltpu.make_async_copy(early, result.at[pl.ds(0, ready)], early_sem)
    diag_copy = pltpu.make_async_copy(diag, diag_out, diag_sem)

    def out_copy(j):
        span = pl.ds(j * BAND, BAND)
        return pltpu.make_async_copy(
            out.at[:, span], result.at[pl.ds(ready, W), span], out_sem.at[j]
        )

    early_copy.start()
    diag_copy.start()
    apply_rows(fock, masked, out, 0, lambda j: out_copy(j).start())
    for j in range(masked.shape[1] // BAND):
        out_copy(j).wait()
    early_copy.wait()
    diag_copy.wait()


def per_device_whole(density, listed, three_centre):
    rows, cols = density.shape
    groups = rows // W
    units = rows // UNIT
    aux_count = three_centre.shape[0]
    aux_group = aux_count * lax.axis_size("col") // groups
    bf16, dma = jnp.bfloat16, pltpu.SemaphoreType.DMA
    in_hbm = pl.BlockSpec(memory_space=pltpu.HBM)
    in_vmem = pl.BlockSpec(memory_space=pltpu.VMEM)
    handed = pl.pallas_call(
        functools.partial(exchange_kernel, aux_group ** (-0.5)),
        out_shape=(
            pltpu.VMEM((rows - W, cols), bf16),
            pltpu.VMEM((W, cols), bf16),
            pltpu.VMEM((W, W), bf16),
            pltpu.VMEM((rows, TILE), jnp.float32),
        ),
        in_specs=[pl.BlockSpec(memory_space=pltpu.SMEM), in_hbm, in_hbm],
        out_specs=(in_vmem,) * 4,
        scratch_shapes=[
            pltpu.VMEM((groups, 2, W, HALF), bf16),
            pltpu.VMEM((groups, 2, W, HALF), bf16),
            pltpu.VMEM((aux_count, W, W), bf16),
            pltpu.VMEM((aux_count // groups, W, HALF), bf16),
            pltpu.VMEM((rows, W), jnp.float32),
            pltpu.VMEM((units, 2, 2, PART, TILE), bf16),
            pltpu.VMEM((units, 2, 2, PART, TILE), bf16),
            pltpu.VMEM((units, 2, PART, TILE), bf16),
            pltpu.VMEM((units, 2, PART, TILE), bf16),
            pltpu.VMEM((rows - W, W), bf16),
            pltpu.VMEM((groups - 1, W, cols), bf16),
            dma((groups,)),
            dma,
            dma((groups,)),
            dma((groups,)),
            dma((groups, 2, W // PIECE)),
            dma((groups,)),
            dma,
            dma((units, 2)),
            dma,
            dma((units, 2)),
            dma,
            dma((units, 2)),
            dma,
            dma((groups,)),
        ],
        compiler_params=pltpu.CompilerParams(
            collective_id=0, has_side_effects=True, vmem_limit_bytes=VMEM_GRANT
        ),
    )(*(pltpu.with_memory_space_constraint(value, pltpu.HBM) for value in (listed, density, three_centre)))
    result, diag = pl.pallas_call(
        apply_kernel,
        out_shape=(
            jax.ShapeDtypeStruct((rows, cols), bf16),
            jax.ShapeDtypeStruct((rows, TILE), jnp.float32),
        ),
        in_specs=[in_vmem] * 4,
        out_specs=(in_hbm, in_hbm),
        scratch_shapes=[pltpu.VMEM((W, cols), bf16), dma, dma((cols // BAND,)), dma],
        compiler_params=pltpu.CompilerParams(vmem_limit_bytes=VMEM_GRANT),
    )(*(pltpu.with_memory_space_constraint(value, pltpu.VMEM) for value in handed))
    return diag, result


def takes_whole(mesh, density, listed, three_centre):
    row_count, col_count = mesh.shape["row"], mesh.shape["col"]
    rows = density.shape[0] // row_count
    cols = density.shape[1] // col_count
    aux_count = three_centre.shape[0] // (row_count * col_count)
    if rows % W or rows < 2 * W or cols % rows or col_count != 4 or col_count * TILE != W:
        return False
    return aux_count % (rows // W) == 0


def solution(mesh):
    placed = (P("row", "col"), P("row", "col"), P(("row", "col"), None, None))

    def mapped(body):
        return jax.shard_map(
            body,
            mesh=mesh,
            in_specs=placed,
            out_specs=(P("row", "col"), P("row", "col")),
            check_vma=False,
        )

    def run(density, listed, three_centre):
        whole = takes_whole(mesh, density, listed, three_centre)
        return mapped(per_device_whole if whole else per_device)(density, listed, three_centre)

    return run
```
